32 devices in a mesh: dp: 4 (over z), expert: 8 (over y, x, core).
Axes of the slice: x: 2, y: 2, z: 4, core: 2. Of those that a mesh axis runs over, the one named last changes fastest.
Arguments:
- grad_parts: bfloat16 [4, 32, 128, 2048], P('dp', 'expert'), may hold values from -6 to 6
- first_moment: float32 [32, 128, 2048], P('expert', None, 'dp'), may hold values from -4 to 4
- second_moment: float32 [32, 128, 2048], P('expert', None, 'dp'), may hold values from 0.05 to 2
- master_weight: float32 [32, 128, 2048], P('expert', None, 'dp'), may hold values from -6 to 6
- old_owner: int32 [28], replicated, may hold values from 0 to 6, as said below
- new_owner: int32 [28], replicated, may hold values from 0 to 7, as said below
Outputs:
- new_master: float32 [48, 128, 2048], P('expert', None, 'dp')
- new_first: float32 [48, 128, 2048], P('expert', None, 'dp')
- new_second: float32 [48, 128, 2048], P('expert', None, 'dp')
- new_params: bfloat16 [48, 128, 2048], P('expert')
The draws below stay inside these ranges and needn't reach their ends.
Inputs may be any that keep to these rules, and one draw needn't show every extreme that they name: `old_owner`: tiles are owned by devices 0 to 6 of the expert axis, exactly 4 each; the other devices own none, and their slots of the old-layout arrays are never read. `new_owner`: each device owns at most 6 tiles and some own exactly 6; the tiles of one old owner go to different new owners.
All inputs are finite; a program needn't handle non-finite values.
Results may differ from the reference program's by a relative error of at most 0.0085.
Values may be sent and summed in bfloat16 or wider, within the bound.
A program may use at most 128 MiB of HBM per device.

```python
import math
import jax
import jax.numpy as jnp
from jax import lax

FF = 2048
TILE_ROWS = 128
OLD_SLOTS = 4
OLD_DEV = 7
NEW_SLOTS = 6
HOT = 1
TILES = 28
N_DP = 4
N_EXPERT = 8


def owner_maps(key):
    key_perm, key_place = jax.random.split(jax.random.fold_in(key, 7))
    shuffle = jax.random.permutation(key_perm, TILES).astype(jnp.int32)
    counter = jnp.arange(TILES, dtype=jnp.int32)
    old_map = jnp.zeros((TILES,), jnp.int32).at[shuffle].set(counter // OLD_SLOTS)
    device_ids = jnp.arange(N_EXPERT, dtype=jnp.int32)
    remaining = TILES - HOT * NEW_SLOTS
    base_load = remaining // (N_EXPERT - HOT)
    extra_load = remaining % (N_EXPERT - HOT)
    load_sizes = jnp.where(device_ids < HOT, NEW_SLOTS, base_load + (device_ids - HOT < extra_load).astype(jnp.int32))
    bounds = jnp.cumsum(load_sizes).astype(jnp.int32)
    position = jnp.sum((counter[:, None] >= bounds[None, :]).astype(jnp.int32), axis=1)
    slot_part = counter // OLD_DEV
    owner_part = counter % OLD_DEV
    tile_ids = shuffle[owner_part * OLD_SLOTS + slot_part]
    relabel = jax.random.permutation(key_place, N_EXPERT).astype(jnp.int32)
    new_map = jnp.zeros((TILES,), jnp.int32).at[tile_ids].set(relabel[position])
    return (old_map, new_map)


def draw_old_owner(key, part):
    return owner_maps(key)[0]


def draw_new_owner(key, part):
    return owner_maps(key)[1]


def block_scale(own_key, dims, shards, least, high):
    gain = 1.0
    for axis_at, shards_of in shards:
        draws = jax.random.uniform(jax.random.fold_in(jax.random.fold_in(own_key, 6), axis_at), (shards_of,), jnp.float32, least / len(shards), high / len(shards))
        gain = gain * jnp.repeat(jnp.exp(draws), dims[axis_at] // shards_of).reshape((-1,) + (1,) * (len(dims) - 1 - axis_at))
    return gain


def noise(key, dims, width, reach, cuts=(), kind=jnp.bfloat16):
    array = jax.random.normal(key, dims, jnp.float32) * width
    if len(cuts) > 0:
        array = block_scale(key, dims, cuts, -0.22, 0.18) * array
    return jnp.clip(array, min=-reach, max=reach).astype(kind)


def setup_inputs(seed: int = 0) -> dict:
    keys = jax.random.split(jax.random.key(seed), 7)
    return {
        "grad_parts": noise(keys[0], (N_DP, N_EXPERT * OLD_SLOTS, TILE_ROWS, FF), 1.0, 6.0, ((0, 4), (1, 8))),
        "first_moment": noise(keys[1], (N_EXPERT * OLD_SLOTS, TILE_ROWS, FF), 0.3, 4.0, ((0, 8), (2, 4)), jnp.float32),
        "second_moment": jnp.clip(jnp.exp(math.log(2.0) - 3.6888794 * jax.random.uniform(keys[2], (N_EXPERT * OLD_SLOTS, TILE_ROWS, FF), jnp.float32) ** block_scale(keys[2], (N_EXPERT * OLD_SLOTS, TILE_ROWS, FF), ((0, 8), (2, 4)), -0.2, 0.2)), 0.05, 2.0),
        "master_weight": noise(keys[3], (N_EXPERT * OLD_SLOTS, TILE_ROWS, FF), 0.5, 6.0, ((0, 8), (2, 4)), jnp.float32),
        "old_owner": draw_old_owner(jax.random.fold_in(keys[6], 71), 0),
        "new_owner": draw_new_owner(jax.random.fold_in(keys[6], 71), 0),
    }


def slot_ranks(owner, count):
    matches = (owner[:, None] == jnp.arange(count, dtype=jnp.int32)[None, :]).astype(jnp.int32)
    before = jnp.cumsum(matches, axis=0) - matches
    return lax.optimization_barrier(jnp.sum(before * matches, axis=1)).astype(jnp.int32)

def adam_step(gradient, moment_one, moment_two, weight):
    moment_one = 0.9 * moment_one + 0.1 * gradient
    moment_two = 0.95 * moment_two + 0.05 * gradient * gradient
    update = moment_one / (1.0 - 0.9 ** 50) / (jnp.sqrt(moment_two / (1.0 - 0.95 ** 50)) + 1e-08)
    weight = weight - 0.05 * (update + 0.1 * weight)
    return (weight, moment_one, moment_two)

def reference(grad_parts, first_moment, second_moment, master_weight, old_owner, new_owner):
    old_rank = slot_ranks(old_owner, N_EXPERT)
    new_rank = slot_ranks(new_owner, N_EXPERT)
    source_rows = (old_owner * OLD_SLOTS + old_rank).astype(jnp.int32)
    target_rows = (new_owner * NEW_SLOTS + new_rank).astype(jnp.int32)
    gradient = jnp.zeros((TILES, TILE_ROWS, FF), jnp.float32)
    for replica in range(N_DP):
        gradient = gradient + grad_parts[replica][source_rows].astype(jnp.float32)
    weight, moment_one, moment_two = adam_step(gradient, first_moment[source_rows], second_moment[source_rows], master_weight[source_rows])
    empty = jnp.zeros((N_EXPERT * NEW_SLOTS, TILE_ROWS, FF), jnp.float32)
    new_master = empty.at[target_rows].set(weight)
    new_first = empty.at[target_rows].set(moment_one)
    new_second = empty.at[target_rows].set(moment_two)
    return (new_master, new_first, new_second, new_master.astype(jnp.bfloat16))
```

```python
import functools

import jax
import jax.numpy as jnp
from jax import lax
from jax.experimental import pallas as pl
from jax.experimental.pallas import tpu as pltpu
from jax.sharding import PartitionSpec as P

MESH = pl.DeviceIdType.MESH
ROWS = 32
AHEAD = 1


def slot_ranks(owner):
    earlier = jnp.tril(jnp.ones((owner.shape[0],) * 2, jnp.bool_), -1)
    return jnp.sum(((owner[:, None] == owner[None, :]) & earlier).astype(jnp.int32), axis=1)


def adam_step(gradient, moment_one, moment_two, weight):
    moment_one = 0.9 * moment_one + 0.1 * gradient
    moment_two = 0.95 * moment_two + 0.05 * gradient * gradient
    update = moment_one / (1.0 - 0.9**50) / (jnp.sqrt(moment_two / (1.0 - 0.95**50)) + 1e-08)
    weight = weight - 0.05 * (update + 0.1 * weight)
    return (weight, moment_one, moment_two)


def kernel(dp, peers, owners, chunks, slot_ref, source_ref, has_ref, g_hbm, m_hbm, v_hbm, w_hbm, *rest):
    outs, params_out, rest = rest[:3], rest[3], rest[4:]
    g, state, part, up, down, stay, params = rest[:7]
    rest = rest[7:]
    fresh, mail, inbox, final = (rest[i * chunks : (i + 1) * chunks] for i in range(4))
    (in_sem, up_send, up_recv, down_send, down_recv, x_send, x_recv,
     gu_send, gu_recv, gd_send, gd_recv, out_sem, params_sem) = rest[4 * chunks :]
    z = lax.axis_index("dp")
    e = lax.axis_index("expert")
    cols = stay.shape[-1]
    new_slots = params.shape[0]
    mine = pl.ds(pl.multiple_of(z * cols, cols), cols)
    owns = e < owners

    loads = [pltpu.make_async_copy(g_hbm.at[0], g, in_sem.at[0])]
    loads += [
        pltpu.make_async_copy(ref, state.at[i], in_sem.at[i + 1])
        for i, ref in enumerate((m_hbm, v_hbm, w_hbm))
    ]
    for load in loads:
        load.start()

    barrier = pltpu.get_barrier_semaphore()
    for step in range(1, peers):
        pl.semaphore_signal(
            barrier, inc=1, device_id={"expert": lax.rem(e + step, peers)}, device_id_type=MESH
        )

    @pl.when(z > 0)
    def _():
        pl.semaphore_signal(barrier, inc=1, device_id={"dp": z - 1}, device_id_type=MESH)

    @pl.when(z < dp - 1)
    def _():
        pl.semaphore_signal(barrier, inc=1, device_id={"dp": z + 1}, device_id_type=MESH)

    inner = (z > 0).astype(jnp.int32) + (z < dp - 1).astype(jnp.int32)
    pl.semaphore_wait(barrier, peers - 1 + inner)
    for load in loads:
        load.wait()

    def rows(c):
        return pl.ds(c * ROWS, ROWS)

    def block(k):
        return pl.ds(k * cols, cols)

    def up_copy(c, k, raw):
        src = g.at[:, rows(c), block(k)] if raw else part.at[k, :, rows(c)]
        return pltpu.make_async_remote_copy(
            src, up.at[k, :, rows(c)], up_send.at[c, k], up_recv.at[c, k],
            device_id={"dp": z + 1}, device_id_type=MESH,
        )

    def down_copy(c, k, raw):
        src = g.at[:, rows(c), block(k)] if raw else part.at[k, :, rows(c)]
        return pltpu.make_async_remote_copy(
            src, down.at[k, :, rows(c)], down_send.at[c, k], down_recv.at[c, k],
            device_id={"dp": z - 1}, device_id_type=MESH,
        )

    def gather_copy(c, k, going_up):
        send, recv = (gu_send, gu_recv) if going_up else (gd_send, gd_recv)
        where = params.at[:, rows(c), block(k)]
        return pltpu.make_async_remote_copy(
            where, where, send.at[c, k], recv.at[c, k],
            device_id={"dp": z + 1 if going_up else z - 1}, device_id_type=MESH,
        )

    def mail_copy(c, to, source):
        return pltpu.make_async_remote_copy(
            mail[c].at[to], inbox[c].at[source], x_send.at[c, to], x_recv.at[c, source],
            device_id={"expert": to}, device_id_type=MESH,
        )

    def first_sends(c):
        @pl.when(owns & (z == 0))
        def _():
            for k in range(dp - 1, 0, -1):
                up_copy(c, k, True).start()

        @pl.when(owns & (z == dp - 1))
        def _():
            for k in range(dp - 1):
                down_copy(c, k, True).start()

    def relay_up(c):
        for k in range(dp - 1, 0, -1):
            @pl.when(owns & (z > 0) & (z < k))
            def _():
                up_copy(c, k, False).wait_recv()
                total = g[:, rows(c), block(k)].astype(jnp.float32) + up[k, :, rows(c)].astype(jnp.float32)
                part[k, :, rows(c)] = total.astype(jnp.bfloat16)
                up_copy(c, k, False).start()

    def relay_down(c):
        for k in range(dp - 1):
            @pl.when(owns & (z < dp - 1) & (z > k))
            def _():
                down_copy(c, k, False).wait_recv()
                total = g[:, rows(c), block(k)].astype(jnp.float32) + down[k, :, rows(c)].astype(jnp.float32)
                part[k, :, rows(c)] = total.astype(jnp.bfloat16)
                down_copy(c, k, False).start()

    def ordered(first, second):
        @pl.when(z * 2 < dp)
        def _():
            first()
            second()

        @pl.when(z * 2 >= dp)
        def _():
            second()
            first()

    def update(c):
        @pl.when(owns)
        def _():
            stay[:, rows(c)] = g[:, rows(c), mine].astype(jnp.float32)
            for k in range(dp):
                @pl.when(z == k)
                def _():
                    if k > 0:
                        up_copy(c, k, False).wait_recv()
                        stay[:, rows(c)] += up[k, :, rows(c)].astype(jnp.float32)
                    if k < dp - 1:
                        down_copy(c, k, False).wait_recv()
                        stay[:, rows(c)] += down[k, :, rows(c)].astype(jnp.float32)
            for slot in range(stay.shape[0]):
                values = adam_step(
                    stay[slot, rows(c)], state[0, slot, rows(c)], state[1, slot, rows(c)], state[2, slot, rows(c)]
                )
                for i, value in enumerate(values):
                    fresh[c][slot, i] = value.astype(jnp.bfloat16)
            for step in range(1, peers):
                to = lax.rem(e + step, peers)
                mail[c][to] = fresh[c][slot_ref[to]]
                mail_copy(c, to, e).start()
            inbox[c][e] = fresh[c][slot_ref[e]]

    def deliver(c):
        for source in range(owners):
            @pl.when(e != source)
            def _():
                mail_copy(c, source, source).wait_recv()
        for slot in range(new_slots):
            present = has_ref[slot] > 0
            for i in range(3):
                value = inbox[c][source_ref[slot], i]
                value = jnp.where(present, value, jnp.zeros_like(value))
                final[c][i, slot] = value.astype(jnp.float32)
                if i == 0:
                    params[slot, rows(c), mine] = value
        for i in range(3):
            pltpu.make_async_copy(final[c].at[i], outs[i].at[:, rows(c)], out_sem.at[c, i]).start()
        for k in range(dp):
            @pl.when(z == k)
            def _():
                if k < dp - 1:
                    gather_copy(c, k, True).start()
                if k > 0:
                    gather_copy(c, k, False).start()

    def spread(c):
        def upward():
            for k in range(dp - 2, -1, -1):
                @pl.when(z > k)
                def _():
                    gather_copy(c, k, True).wait_recv()

                    @pl.when(z < dp - 1)
                    def _():
                        gather_copy(c, k, True).start()

        def downward():
            for k in range(1, dp):
                @pl.when(z < k)
                def _():
                    gather_copy(c, k, False).wait_recv()

                    @pl.when(z > 0)
                    def _():
                        gather_copy(c, k, False).start()

        ordered(upward, downward)
        pltpu.make_async_copy(params.at[:, rows(c)], params_out.at[:, rows(c)], params_sem.at[c]).start()

    for c in range(min(AHEAD, chunks)):
        first_sends(c)
    for c in range(chunks + 2):
        if c < chunks:
            if c + AHEAD < chunks:
                first_sends(c + AHEAD)
            ordered(functools.partial(relay_up, c), functools.partial(relay_down, c))
            update(c)
        if 1 <= c <= chunks:
            deliver(c - 1)
        if c >= 2:
            spread(c - 2)

    for c in range(chunks):
        @pl.when(owns)
        def _():
            for k in range(1, dp):
                @pl.when(z < k)
                def _():
                    up_copy(c, k, False).wait_send()
            for k in range(dp - 1):
                @pl.when(z > k)
                def _():
                    down_copy(c, k, False).wait_send()
            for step in range(1, peers):
                mail_copy(c, lax.rem(e + step, peers), e).wait_send()
        for k in range(dp):
            @pl.when((z >= k) & (z < dp - 1))
            def _():
                gather_copy(c, k, True).wait_send()

            @pl.when((z <= k) & (z > 0))
            def _():
                gather_copy(c, k, False).wait_send()
        for i in range(3):
            pltpu.make_async_copy(final[c].at[i], outs[i].at[:, rows(c)], out_sem.at[c, i]).wait()
        pltpu.make_async_copy(params.at[:, rows(c)], params_out.at[:, rows(c)], params_sem.at[c]).wait()


def shards(grad_parts, first_moment, second_moment, master_weight, old_owner, new_owner):
    dp = lax.axis_size("dp")
    peers = lax.axis_size("expert")
    device = lax.axis_index("expert")
    old_slots, tile_rows, cols = first_moment.shape
    owners = old_owner.shape[0] // old_slots
    new_slots = min(old_slots + old_slots // 2, peers - peers // 5)
    chunks = tile_rows // ROWS
    old_rank = slot_ranks(old_owner)
    new_rank = slot_ranks(new_owner)
    targets = jnp.arange(peers, dtype=jnp.int32)
    outgoing = (old_owner == device)[None, :] & (new_owner[None, :] == targets[:, None])
    send_slot = jnp.sum(jnp.where(outgoing, old_rank[None, :], 0), axis=1)
    slot_ids = jnp.arange(new_slots, dtype=jnp.int32)
    wanted = (new_owner == device)[None, :] & (new_rank[None, :] == slot_ids[:, None])
    recv_has = jnp.sum(wanted.astype(jnp.int32), axis=1)
    recv_source = jnp.sum(jnp.where(wanted, old_owner[None, :], 0), axis=1)

    bf16, f32 = jnp.bfloat16, jnp.float32
    dma = pltpu.SemaphoreType.DMA
    any_space = pl.BlockSpec(memory_space=pl.ANY)
    smem = pl.BlockSpec(memory_space=pltpu.SMEM)
    master = jax.ShapeDtypeStruct((new_slots, tile_rows, cols), f32)
    scratch = [
        pltpu.VMEM((old_slots, tile_rows, dp * cols), bf16),
        pltpu.VMEM((3, old_slots, tile_rows, cols), f32),
        pltpu.VMEM((dp, old_slots, tile_rows, cols), bf16),
        pltpu.VMEM((dp, old_slots, tile_rows, cols), bf16),
        pltpu.VMEM((dp, old_slots, tile_rows, cols), bf16),
        pltpu.VMEM((old_slots, tile_rows, cols), f32),
        pltpu.VMEM((new_slots, tile_rows, dp * cols), bf16),
    ]
    scratch += [pltpu.VMEM((old_slots, 3, ROWS, cols), bf16)] * chunks
    scratch += [pltpu.VMEM((peers, 3, ROWS, cols), bf16)] * chunks
    scratch += [pltpu.VMEM((peers, 3, ROWS, cols), bf16)] * chunks
    scratch += [pltpu.VMEM((3, new_slots, ROWS, cols), f32)] * chunks
    scratch += [dma((4,))] + [dma((chunks, dp))] * 4 + [dma((chunks, peers))] * 2
    scratch += [dma((chunks, dp))] * 4 + [dma((chunks, 3)), dma((chunks,))]
    return pl.pallas_call(
        functools.partial(kernel, dp, peers, owners, chunks),
        out_shape=(master,) * 3
        + (jax.ShapeDtypeStruct((new_slots, tile_rows, dp * cols), bf16),),
        in_specs=[smem] * 3 + [any_space] * 4,
        out_specs=(any_space,) * 4,
        scratch_shapes=scratch,
        compiler_params=pltpu.CompilerParams(
            collective_id=0, has_side_effects=True, vmem_limit_bytes=60 * 2**20
        ),
    )(send_slot, recv_source, recv_has, grad_parts, first_moment, second_moment, master_weight)


def solution(mesh):
    placed = (
        P("dp", "expert", None, None),
        P("expert", None, "dp"),
        P("expert", None, "dp"),
        P("expert", None, "dp"),
        P(),
        P(),
    )
    return jax.shard_map(
        shards,
        mesh=mesh,
        in_specs=placed,
        out_specs=(
            P("expert", None, "dp"),
            P("expert", None, "dp"),
            P("expert", None, "dp"),
            P("expert", None, None),
        ),
        check_vma=False,
    )
```

```python
import functools

import jax
import jax.numpy as jnp
from jax import lax
from jax.experimental import pallas as pl
from jax.experimental.pallas import tpu as pltpu
from jax.sharding import PartitionSpec as P

MESH = pl.DeviceIdType.MESH
ROWS = 16
AHEAD = 1
HOP = 1
MAIL = 2
WIDE = 2
PLAN = (1, 0)


def early(c):
    return PLAN[c % len(PLAN)] == 1


def adam_step(gradient, moment_one, moment_two, weight):
    moment_one = 0.9 * moment_one + 0.1 * gradient
    moment_two = 0.95 * moment_two + 0.05 * gradient * gradient
    update = moment_one / (1.0 - 0.9**50) / (jnp.sqrt(moment_two / (1.0 - 0.95**50)) + 1e-08)
    weight = weight - 0.05 * (update + 0.1 * weight)
    return (weight, moment_one, moment_two)


def kernel(dp, peers, owners, chunks, old_ref, new_ref, g_hbm, m_hbm, v_hbm, w_hbm, *rest):
    outs, params, rest = rest[:3], rest[3], rest[4:]
    g, state, part, up, down, stay = rest[:6]
    rest = rest[6:]
    fresh, mail, inbox, wide, wide_mail, wide_inbox = (rest[i * chunks : (i + 1) * chunks] for i in range(6))
    (in_sem, up_send, up_recv, down_send, down_recv, x_send, x_recv, w_send, w_recv,
     gu_send, gu_recv, gd_send, gd_recv) = rest[6 * chunks :]
    z = lax.axis_index("dp")
    e = lax.axis_index("expert")
    cols = stay.shape[-1]
    new_slots = params.shape[0]
    mine = pl.ds(pl.multiple_of(z * cols, cols), cols)
    owns = e < owners

    loads = [pltpu.make_async_copy(g_hbm.at[0], g, in_sem.at[0])]
    loads += [
        pltpu.make_async_copy(ref, state.at[i], in_sem.at[i + 1])
        for i, ref in enumerate((m_hbm, v_hbm, w_hbm))
    ]
    for load in loads:
        load.start()

    barrier = pltpu.get_barrier_semaphore()
    for step in range(1, peers):
        pl.semaphore_signal(
            barrier, inc=1, device_id={"expert": lax.rem(e + step, peers)}, device_id_type=MESH
        )

    @pl.when(z > 0)
    def _():
        pl.semaphore_signal(barrier, inc=1, device_id={"dp": z - 1}, device_id_type=MESH)

    @pl.when(z < dp - 1)
    def _():
        pl.semaphore_signal(barrier, inc=1, device_id={"dp": z + 1}, device_id_type=MESH)

    inner = (z > 0).astype(jnp.int32) + (z < dp - 1).astype(jnp.int32)
    pl.semaphore_wait(barrier, peers - 1 + inner)
    for load in loads:
        load.wait()

    tiles = old_ref.shape[0]
    targets = [lax.rem(e + step, peers) for step in range(peers)]

    def route(tile, carry):
        sent, taken, slots, sources = carry
        old, new = old_ref[tile], new_ref[tile]
        leaves, comes = old == e, new == e
        slots = tuple(jnp.where(leaves & (new == to), sent, slot) for to, slot in zip(targets, slots))
        sources = tuple(
            jnp.where(comes & (taken == slot), old, source) for slot, source in enumerate(sources)
        )
        return sent + leaves.astype(jnp.int32), taken + comes.astype(jnp.int32), slots, sources

    def rows(c):
        return pl.ds(c * ROWS, ROWS)

    def block(k):
        return pl.ds(k * cols, cols)

    def up_copy(c, k, raw):
        src = g.at[:, rows(c), block(k)] if raw else part.at[k, :, rows(c)]
        return pltpu.make_async_remote_copy(
            src, up.at[k, :, rows(c)], up_send.at[c, k], up_recv.at[c, k],
            device_id={"dp": z + 1}, device_id_type=MESH,
        )

    def down_copy(c, k, raw):
        src = g.at[:, rows(c), block(k)] if raw else part.at[k, :, rows(c)]
        return pltpu.make_async_remote_copy(
            src, down.at[k, :, rows(c)], down_send.at[c, k], down_recv.at[c, k],
            device_id={"dp": z - 1}, device_id_type=MESH,
        )

    def gather_copy(c, k, going_up):
        send, recv = (gu_send, gu_recv) if going_up else (gd_send, gd_recv)
        where = wide[c].at[:, :, block(k)] if early(c) else params.at[:, rows(c), block(k)]
        return pltpu.make_async_remote_copy(
            where, where, send.at[c, k], recv.at[c, k],
            device_id={"dp": z + 1 if going_up else z - 1}, device_id_type=MESH,
        )

    def mail_copy(c, to, source):
        return pltpu.make_async_remote_copy(
            mail[c].at[to], inbox[c].at[source], x_send.at[c, to], x_recv.at[c, source],
            device_id={"expert": to}, device_id_type=MESH,
        )

    def wide_copy(c, to, source):
        return pltpu.make_async_remote_copy(
            wide_mail[c].at[to], wide_inbox[c].at[source], w_send.at[c, to], w_recv.at[c, source],
            device_id={"expert": to}, device_id_type=MESH,
        )

    def first_sends(c):
        @pl.when(owns & (z == 0))
        def _():
            for k in range(dp - 1, 0, -1):
                up_copy(c, k, True).start()

        @pl.when(owns & (z == dp - 1))
        def _():
            for k in range(dp - 1):
                down_copy(c, k, True).start()

    def relay_up(c, at):
        for k in range(dp - 1, at, -1):
            up_copy(c, k, False).wait_recv()
            total = g[:, rows(c), block(k)].astype(jnp.float32) + up[k, :, rows(c)].astype(jnp.float32)
            part[k, :, rows(c)] = total.astype(jnp.bfloat16)
            up_copy(c, k, False).start()

    def relay_down(c, at):
        for k in range(at):
            down_copy(c, k, False).wait_recv()
            total = g[:, rows(c), block(k)].astype(jnp.float32) + down[k, :, rows(c)].astype(jnp.float32)
            part[k, :, rows(c)] = total.astype(jnp.bfloat16)
            down_copy(c, k, False).start()

    def relay(c, at, going_up):
        @pl.when(owns & (z == at))
        def _():
            (relay_up if going_up else relay_down)(c, at)

    def update(c):
        @pl.when(owns)
        def _():
            stay[...] = g[:, rows(c), mine].astype(jnp.float32)
            for k in range(dp):
                @pl.when(z == k)
                def _():
                    if k > 0:
                        up_copy(c, k, False).wait_recv()
                        stay[...] += up[k, :, rows(c)].astype(jnp.float32)
                    if k < dp - 1:
                        down_copy(c, k, False).wait_recv()
                        stay[...] += down[k, :, rows(c)].astype(jnp.float32)
            for slot in range(stay.shape[0]):
                values = adam_step(
                    stay[slot], state[0, slot, rows(c)], state[1, slot, rows(c)], state[2, slot, rows(c)]
                )
                values = [value.astype(jnp.bfloat16) for value in values]
                if early(c):
                    wide[c][slot, :, mine] = values.pop(0)
                for i, value in enumerate(values):
                    fresh[c][slot, i] = value
            if early(c):
                gather(c)
            for to, slot in zip(targets[1:], slots[1:]):
                mail[c][to] = fresh[c][slot]
                mail_copy(c, to, e).start()
            inbox[c][e] = fresh[c][slots[0]]

    def gather(c):
        for k in range(dp):
            @pl.when(z == k)
            def _():
                if k < dp - 1:
                    gather_copy(c, k, True).start()
                if k > 0:
                    gather_copy(c, k, False).start()

    def forward(c, hop):
        for at in range(1, dp - 1):
            @pl.when((owns & (z == at)) if early(c) else (z == at))
            def _():
                for k, going_up in ((at - hop, True), (at + hop, False)):
                    if 0 <= k < dp:
                        gather_copy(c, k, going_up).wait_recv()
                        gather_copy(c, k, going_up).start()

    def gathered(c):
        @pl.when(z == dp - 1)
        def _():
            for k in range(dp - 1):
                gather_copy(c, k, True).wait_recv()

        @pl.when(z == 0)
        def _():
            for k in range(1, dp):
                gather_copy(c, k, False).wait_recv()

    def post_wide(c):
        @pl.when(owns)
        def _():
            gathered(c)
            for to, slot in zip(targets[1:], slots[1:]):
                wide_mail[c][to] = wide[c][slot]
                wide_copy(c, to, e).start()
            wide_inbox[c][e] = wide[c][slots[0]]

    def deliver(c):
        for source in range(owners):
            @pl.when(e != source)
            def _():
                mail_copy(c, source, source).wait_recv()
                if early(c):
                    wide_copy(c, source, source).wait_recv()

        for slot in range(new_slots):
            present = taken > slot

            def kept(value):
                return jnp.where(present, value, jnp.zeros_like(value))

            if early(c):
                params[slot, rows(c)] = kept(wide_inbox[c][sources[slot]])
                outs[0][slot, rows(c)] = kept(wide_inbox[c][sources[slot], :, mine]).astype(jnp.float32)
            else:
                value = kept(inbox[c][sources[slot], 0])
                params[slot, rows(c), mine] = value
                outs[0][slot, rows(c)] = value.astype(jnp.float32)
            first = 0 if early(c) else 1
            for i in range(2):
                value = kept(inbox[c][sources[slot], first + i])
                outs[i + 1][slot, rows(c)] = value.astype(jnp.float32)
        if not early(c):
            gather(c)

    for c in range(min(AHEAD, chunks)):
        first_sends(c)
    zero = jnp.int32(0)
    _, taken, slots, sources = lax.fori_loop(
        0, tiles, route, (zero, zero, (zero,) * peers, (zero,) * new_slots)
    )
    slots = tuple(jnp.minimum(slot, stay.shape[0] - 1) for slot in slots)
    sources = tuple(jnp.minimum(source, owners - 1) for source in sources)
    jobs = []
    for c in range(chunks):
        if c >= AHEAD:
            jobs.append((c - AHEAD + 1, c, first_sends, (c,)))
        for at in range(1, dp - 1):
            jobs.append((c + at * HOP, c, relay, (c, at, True)))
            jobs.append((c + (dp - 1 - at) * HOP, c, relay, (c, at, False)))
        now = c + (dp - 1) * HOP
        jobs.append((now, c, update, (c,)))
        if not early(c):
            now += MAIL
            jobs.append((now, c, deliver, (c,)))
        for hop in range(1, dp - 1):
            jobs.append((now + hop * HOP, c, forward, (c, hop)))
        now += (dp - 1) * HOP
        if early(c):
            jobs.append((now, c, post_wide, (c,)))
            jobs.append((now + WIDE, c, deliver, (c,)))
        else:
            jobs.append((now, c, gathered, (c,)))
    for _, _, job, args in sorted(jobs, key=lambda item: item[:2]):
        job(*args)

    for c in range(chunks):
        for k in range(dp):
            reach = owns if early(c) else True

            @pl.when(reach & (z >= k) & (z < dp - 1))
            def _():
                gather_copy(c, k, True).wait_send()

            @pl.when(reach & (z <= k) & (z > 0))
            def _():
                gather_copy(c, k, False).wait_send()

        @pl.when(owns)
        def _():
            for k in range(1, dp):
                @pl.when(z < k)
                def _():
                    up_copy(c, k, False).wait_send()
            for k in range(dp - 1):
                @pl.when(z > k)
                def _():
                    down_copy(c, k, False).wait_send()
            for to in targets[1:]:
                mail_copy(c, to, e).wait_send()
                if early(c):
                    wide_copy(c, to, e).wait_send()


def shards(grad_parts, first_moment, second_moment, master_weight, old_owner, new_owner):
    dp = lax.axis_size("dp")
    peers = lax.axis_size("expert")
    old_slots, tile_rows, cols = first_moment.shape
    owners = old_owner.shape[0] // old_slots
    new_slots = min(old_slots + old_slots // 2, peers - peers // 5)
    chunks = tile_rows // ROWS
    bf16, f32 = jnp.bfloat16, jnp.float32
    dma = pltpu.SemaphoreType.DMA
    any_space = pl.BlockSpec(memory_space=pl.ANY)
    smem = pl.BlockSpec(memory_space=pltpu.SMEM)
    master = jax.ShapeDtypeStruct((new_slots, tile_rows, cols), f32)
    scratch = [
        pltpu.VMEM((old_slots, tile_rows, dp * cols), bf16),
        pltpu.VMEM((3, old_slots, tile_rows, cols), f32),
        pltpu.VMEM((dp, old_slots, tile_rows, cols), bf16),
        pltpu.VMEM((dp, old_slots, tile_rows, cols), bf16),
        pltpu.VMEM((dp, old_slots, tile_rows, cols), bf16),
        pltpu.VMEM((old_slots, ROWS, cols), f32),
    ]
    first = [early(c) for c in range(chunks)]
    kept = [2 if flag else 3 for flag in first]
    width = [dp * cols if flag else 128 for flag in first]
    span = [ROWS if flag else 16 for flag in first]
    scratch += [pltpu.VMEM((old_slots, n, ROWS, cols), bf16) for n in kept]
    scratch += [pltpu.VMEM((peers, n, ROWS, cols), bf16) for n in kept]
    scratch += [pltpu.VMEM((owners, n, ROWS, cols), bf16) for n in kept]
    scratch += [pltpu.VMEM((old_slots, r, n), bf16) for r, n in zip(span, width)]
    scratch += [pltpu.VMEM((peers, r, n), bf16) for r, n in zip(span, width)]
    scratch += [pltpu.VMEM((owners, r, n), bf16) for r, n in zip(span, width)]
    scratch += [dma((4,))] + [dma((chunks, dp))] * 4 + [dma((chunks, peers))] * 4
    scratch += [dma((chunks, dp))] * 4
    results = new_slots * tile_rows * cols * (12 + 2 * dp)
    return pl.pallas_call(
        functools.partial(kernel, dp, peers, owners, chunks),
        out_shape=(master,) * 3
        + (jax.ShapeDtypeStruct((new_slots, tile_rows, dp * cols), bf16),),
        in_specs=[smem] * 2 + [any_space] * 4,
        out_specs=(pl.BlockSpec(memory_space=pltpu.VMEM),) * 4,
        scratch_shapes=scratch,
        compiler_params=pltpu.CompilerParams(
            collective_id=0, has_side_effects=True, vmem_limit_bytes=67043328 - results - 2**19
        ),
    )(old_owner, new_owner, grad_parts, first_moment, second_moment, master_weight)


def solution(mesh):
    placed = (
        P("dp", "expert", None, None),
        P("expert", None, "dp"),
        P("expert", None, "dp"),
        P("expert", None, "dp"),
        P(),
        P(),
    )
    return jax.shard_map(
        shards,
        mesh=mesh,
        in_specs=placed,
        out_specs=(
            P("expert", None, "dp"),
            P("expert", None, "dp"),
            P("expert", None, "dp"),
            P("expert", None, None),
        ),
        check_vma=False,
    )
```
